32 devices in a mesh: dp: 16 (over z, y, core), vocab: 2 (over x).
Axes of the slice: x: 2, y: 2, z: 4, core: 2. Of those that a mesh axis runs over, the one named last changes fastest.
Arguments:
- hidden: bfloat16 [768, 8192], P(None, 'dp')
- lengths: int32 [24], replicated, may hold values from 8 to 32
- positive: int32 [4], replicated, may hold values from 0 to 19, as said below
- norm_gain: bfloat16 [8192], P('dp'), may hold values from 0.099609375 to 1.8984375
- head: bfloat16 [8192, 98304], P(None, ('dp', 'vocab')), may hold values from -0.0625 to 0.0625
Outputs:
- loss: float32 [], replicated
- head_grad: bfloat16 [8192, 98304], P(None, ('dp', 'vocab'))
The draws below stay inside these ranges and needn't reach their ends.
Inputs may be any that keep to these rules, and one draw needn't show every extreme that they name: The queries' positive passages are all different.
All inputs are finite; a program needn't handle non-finite values.
Results may differ from the reference program's by a relative error of at most 0.008.
Values may be sent and summed in bfloat16 or wider, within the bound.
No kernel may reach another device: no remote copies, remote signals or barrier semaphores. Data moves between devices by JAX's collectives and lax.ppermute only.
A program may use at most 256 MiB of HBM per device.

```python
import math
import jax
import jax.numpy as jnp
from jax import lax

D = 8192
VOCAB = 98304
SEQ = 32
NQ = 4
NP = 20
SEQS = 24
TOKENS = 768


def draw_hidden(key, part):
    first, second = jax.random.split(key, 2)
    columns = jnp.arange(D, dtype=jnp.float32) / max(D - 1, 1)
    spread = jax.random.uniform(second, (1, D), jnp.float32, 1.0, 2.0)
    col_scale = jnp.exp(jnp.log(3.0) * columns)[None, :] * spread
    values = jnp.clip(jax.random.normal(first, (TOKENS, D), jnp.float32), -6.0, 6.0) * col_scale
    return values.astype(jnp.bfloat16)


def draw_positive(key, part):
    order = jax.random.permutation(jax.random.fold_in(key, 17), jnp.arange(NP, dtype=jnp.int32))
    return order[:NQ].astype(jnp.int32)


def with_ends(array, key, smallest, high):
    spot = [jax.random.randint(jax.random.fold_in(key, axis), (), 0, length) for axis, length in enumerate(array.shape)]
    main_axis = array.shape.index(max(array.shape))
    beside = spot[:main_axis] + [(spot[main_axis] + 1) % array.shape[main_axis]] + spot[main_axis + 1:]
    return array.at[tuple(spot)].set(smallest).at[tuple(beside)].set(high)


def level_of(stream_key, dims, cuts, smallest, top_value):
    gain, own = 1.0, jax.random.fold_in(stream_key, 6)
    for position, shards_of in cuts:
        draws = jnp.exp(jax.random.uniform(jax.random.fold_in(own, position), (shards_of,), jnp.float32, smallest / len(cuts), top_value / len(cuts)))
        gain = gain * jnp.repeat(draws, dims[position] // shards_of).reshape([-1 if axis == position else 1 for axis in range(len(dims))])
    return gain


def gaussian(stream_key, shape, scale, most, cuts=(), held_as=jnp.bfloat16):
    drawn = jax.random.normal(stream_key, shape, jnp.float32) * scale
    if len(cuts) > 0:
        drawn = level_of(stream_key, shape, cuts, -0.22, 0.18) * drawn
    return jnp.clip(drawn, min=-most, max=most).astype(held_as)


def setup_inputs(seed: int = 0) -> dict:
    arg_keys = jax.random.split(jax.random.key(seed), 6)
    hidden = draw_hidden(jax.random.fold_in(arg_keys[5], 71), 0)
    lengths = with_ends(jax.random.randint(arg_keys[1], (SEQS,), SEQ // 4, SEQ + 1), jax.random.fold_in(arg_keys[1], 1), SEQ // 4, SEQ).astype(jnp.int32)
    positive = draw_positive(jax.random.fold_in(arg_keys[5], 71), 0)
    norm_gain = jnp.clip(1.0 + 0.18 * jax.random.normal(arg_keys[3], (D,), jnp.float32), 0.099609375, 1.8984375).astype(jnp.bfloat16)
    head = gaussian(arg_keys[4], (D, VOCAB), D ** -0.5, 0.0625, ((1, 32),))
    return dict(hidden=hidden, lengths=lengths, positive=positive, norm_gain=norm_gain, head=head)


def reference(hidden, lengths, positive, norm_gain, head):
    seqs = lengths.shape[0]
    values = hidden.astype(jnp.float32)
    mean_sq = lax.optimization_barrier(jnp.mean(values * values, axis=1, keepdims=True))
    normed = (values * lax.rsqrt(mean_sq + 1e-05) * norm_gain.astype(jnp.float32)[None, :]).astype(jnp.bfloat16)
    valid = (jnp.arange(SEQ, dtype=jnp.int32)[None, :] < lengths[:, None]).astype(jnp.float32)
    counts = lengths.astype(jnp.float32)
    dense = lax.optimization_barrier(jnp.sum(normed.astype(jnp.float32).reshape(seqs, SEQ, D) * valid[:, :, None], axis=1)) / counts[:, None]
    logits = jnp.dot(normed, head, preferred_element_type=jnp.float32)
    ramp = jax.nn.relu(logits)
    sat = jnp.log(1.0 + ramp * ramp)
    expo = jnp.exp(sat / 0.25).reshape(seqs, SEQ, VOCAB) * valid[:, :, None]
    total = lax.optimization_barrier(jnp.sum(expo, axis=1))
    sparse = 0.25 * jnp.log(total / counts[:, None])
    root_v = math.sqrt(VOCAB)
    sq_part = sparse[:NQ]
    sp_part = sparse[NQ:]
    scores = jnp.dot(sq_part, sp_part.T, precision=lax.Precision.HIGHEST) / root_v
    scores = scores + jnp.dot(dense[:NQ], dense[NQ:].T, precision=lax.Precision.HIGHEST) * (4.0 / math.sqrt(D))
    onehot = jnp.arange(NP, dtype=jnp.int32)[None, :] == positive[:, None]
    pos_score = lax.optimization_barrier(jnp.sum(jnp.where(onehot, scores, 0.0), axis=1, keepdims=True))
    diff = scores - pos_score
    loss = jnp.sum(jnp.where(onehot, 0.0, jax.nn.softplus(diff)))
    sig = jnp.where(onehot, 0.0, jax.nn.sigmoid(diff))
    gscore = sig - onehot.astype(jnp.float32) * lax.optimization_barrier(jnp.sum(sig, axis=1, keepdims=True))
    grad_q = jnp.dot(gscore, sp_part, precision=lax.Precision.HIGHEST) / root_v
    grad_p = jnp.dot(gscore.T, sq_part, precision=lax.Precision.HIGHEST) / root_v
    gsparse = jnp.concatenate([grad_q, grad_p], axis=0)
    weights = expo / total[:, None, :]
    slope = (2.0 * ramp / (1.0 + ramp * ramp)).reshape(seqs, SEQ, VOCAB)
    glogits = (gsparse[:, None, :] * weights * slope).reshape(seqs * SEQ, VOCAB).astype(jnp.bfloat16)
    head_grad = lax.dot_general(normed, glogits, (((0,), (0,)), ((), ())), preferred_element_type=jnp.float32)
    return (loss, head_grad.astype(jnp.bfloat16))
```

```python
import functools
import math

import jax
import jax.numpy as jnp
import numpy as np
from jax import lax
from jax.experimental import pallas as pl
from jax.experimental.pallas import tpu as pltpu
from jax.sharding import PartitionSpec as P

SEQ = 32
NQ = 4
NP = 20
SEQ_ROWS = 32
EXTRA = 16
WINDOW = SEQ + 8
HI = lax.Precision.HIGHEST
MIB = 1024 * 1024


def split3(x):
    a = x.astype(jnp.bfloat16)
    rest = x - a.astype(jnp.float32)
    b = rest.astype(jnp.bfloat16)
    c = (rest - b.astype(jnp.float32)).astype(jnp.bfloat16)
    return a, b, c


def dot(a, b):
    return jnp.dot(a, b, preferred_element_type=jnp.float32)


def butterfly(x, sizes):
    for axis, size in sizes:
        bit = 1
        while bit < size:
            x = x + lax.ppermute(x, axis, [(j, j ^ bit) for j in range(size)])
            bit *= 2
    return x


def vmem(shape, index, **kw):
    return pl.BlockSpec(shape, index, **kw)


def once():
    return dict(pipeline_mode=pl.Buffered(1))


def pack_kernel(slots, bounds, hidden, gain, pay):
    tokens, width = hidden.shape
    per = -(-slots // width)
    token = lax.broadcasted_iota(jnp.int32, (8, tokens), 1)
    seq, place = token // SEQ, token % SEQ
    target = jnp.full((8, tokens), -1, jnp.int32)
    for s in range(tokens // SEQ):
        start, end = bounds[0, s], bounds[1, s]
        target = jnp.where((seq == s) & (place < end - start), start + place, target)
    slot = lax.broadcasted_iota(jnp.int32, (slots, tokens), 0)
    pick = jnp.where(slot == target[:1], 1.0, 0.0).astype(jnp.bfloat16)
    packed = dot(pick, hidden[...])
    pay[:slots, :] = (packed * gain[...].astype(jnp.float32).reshape(1, width)).astype(jnp.bfloat16)
    squares = lax.dot_general(
        jnp.ones((8, width), jnp.float32), packed * packed, (((1,), (1,)), ((), ())),
        precision=HI, preferred_element_type=jnp.float32,
    )
    row = lax.broadcasted_iota(jnp.int32, (EXTRA, width), 0)
    extra = jnp.zeros((EXTRA, width), jnp.float32)
    for q in range(per):
        lanes = squares[:1, q * width : min((q + 1) * width, slots)]
        if lanes.shape[1] < width:
            lanes = jnp.concatenate([lanes, jnp.zeros((1, width - lanes.shape[1]), jnp.float32)], axis=1)
        for i, v in enumerate(split3(lanes)):
            extra = jnp.where(row == 3 * q + i, v.astype(jnp.float32), extra)
    pay[slots:, :] = extra.astype(jnp.bfloat16)


def pack(slots, bounds, hidden, gain):
    tokens, width = hidden.shape
    return pl.pallas_call(
        functools.partial(pack_kernel, slots),
        out_shape=jax.ShapeDtypeStruct((slots + EXTRA, width), jnp.bfloat16),
        grid_spec=pltpu.PrefetchScalarGridSpec(
            num_scalar_prefetch=1,
            grid=(1,),
            in_specs=[
                vmem((tokens, width), lambda i, b: (0, 0)),
                vmem((width,), lambda i, b: (0,)),
            ],
            out_specs=vmem((slots + EXTRA, width), lambda i, b: (0, 0)),
        ),
        compiler_params=pltpu.CompilerParams(vmem_limit_bytes=32 * MIB),
        cost_estimate=pl.CostEstimate(
            flops=2 * slots * tokens * width, bytes_accessed=2 * (tokens + slots) * width, transcendentals=0
        ),
        name="pack",
    )(bounds, hidden, gain)


def take(slots, at, pieces, heads, acc, sums_in, sums, kept, sem):
    width = heads[0].shape[0]
    copies = []
    for piece in pieces:
        copies.append(
            pltpu.make_async_copy(piece.at[:slots, :], kept.at[:, pl.ds(at, piece.shape[1])], sem.at[len(copies)])
        )
        at += piece.shape[1]

    @pl.when(pl.program_id(0) == 0)
    def _():
        for copy in copies:
            copy.start()
        extra = jnp.zeros(sums.shape, jnp.float32) if sums_in is None else sums_in[...]
        for piece in pieces:
            for h in range(piece.shape[1] // width):
                extra = extra + piece[slots:, h * width : (h + 1) * width].astype(jnp.float32)
        sums[...] = extra

    heads = list(heads)
    for piece in pieces:
        rows = [heads.pop(0)[...] for _ in range(piece.shape[1] // width)]
        part = dot(piece[:slots, :], rows[0] if len(rows) == 1 else jnp.concatenate(rows, axis=0))
        acc = part if acc is None else acc + part

    @pl.when(pl.program_id(0) == pl.num_programs(0) - 1)
    def _():
        for copy in copies:
            copy.wait()

    return acc


def lanes_of(block):
    return pl.ds(pl.multiple_of(pl.program_id(0) * block, block), block)


def partial_kernel(slots, at, n_pieces, n_heads, has_before, ids, bounds, *refs):
    pieces, refs = refs[:n_pieces], refs[n_pieces:]
    heads, refs = refs[:n_heads], refs[n_heads:]
    acc_in, sums_in, _, acc, sums, kept, sem = refs if has_before else (None, None, None, *refs)
    lanes = lanes_of(heads[0].shape[1])
    before = acc_in[:, lanes] if has_before else None
    acc[:, lanes] = take(slots, at, pieces, heads, before, sums_in, sums, kept, sem)


def members(slots, spans):
    slot = lax.broadcasted_iota(jnp.int32, (slots, 128), 0).astype(jnp.float32)
    return (slot >= spans[0:1, :]) & (slot < spans[1:2, :])


def last_kernel(slots, at, n_pieces, n_heads, model_width, vocab, ids, bounds, *refs):
    pieces, refs = refs[:n_pieces], refs[n_pieces:]
    heads, refs = refs[:n_heads], refs[n_heads:]
    acc_in, sums_in, _, spans, own, acc, sums, kept, grown, total, sparse, scores, sem, scale, expo = refs
    width, block = heads[0].shape
    per = -(-slots // width)
    seqs = bounds.shape[1]
    lanes = lanes_of(block)
    x = take(slots, at, pieces, heads, acc_in[:, lanes], sums_in, sums, kept, sem)

    @pl.when(pl.program_id(0) == 0)
    def _():
        rows = [sums[3 * q : 3 * q + 1] + sums[3 * q + 1 : 3 * q + 2] + sums[3 * q + 2 : 3 * q + 3] for q in range(per)]
        line = jnp.concatenate(rows, axis=1) if per > 1 else rows[0]
        line = lax.rsqrt(line / model_width + 1e-05)
        scale[...] = jnp.transpose(jnp.broadcast_to(line, (128, per * width)))
        total[...] = jnp.ones(total.shape, jnp.float32)
        sparse[...] = jnp.ones(sparse.shape, jnp.float32)

    by = scale[:slots, :]
    for i in range(block // 128):
        part = slice(i * 128, (i + 1) * 128)
        ramp = jnp.maximum(x[:, part] * by, 0.0)
        one = 1.0 + ramp * ramp
        two = one * one
        expo[:slots, part] = two * two
        grown[:, part] = ramp * one * two * by

    def add(s, carry):
        start, end = bounds[0, s], bounds[1, s]
        base = pl.multiple_of((start // 8) * 8, 8)
        row = base + lax.broadcasted_iota(jnp.int32, (WINDOW, 128), 0)
        inside = (row >= start) & (row < end)
        parts = [
            jnp.sum(jnp.where(inside, expo[pl.ds(base, WINDOW), i * 128 : (i + 1) * 128], 0.0), axis=0, keepdims=True)
            for i in range(block // 128)
        ]
        line = jnp.concatenate(parts, axis=1)
        total[pl.ds(s, 1), lanes] = line
        sparse[pl.ds(s, 1), lanes] = line / (end - start).astype(jnp.float32)
        return carry

    lax.fori_loop(0, seqs, add, 0)

    @pl.when(pl.program_id(0) == pl.num_programs(0) - 1)
    def _():
        sparse[...] = 0.25 * jnp.log(sparse[...])
        pairs = lax.dot_general(
            sparse[...], sparse[...], (((1,), (1,)), ((), ())), precision=HI, preferred_element_type=jnp.float32
        ) / math.sqrt(vocab)
        weight = jnp.where(members(slots, spans[...]), by / spans[2:3, :], 0.0)
        dense = lax.dot_general(
            weight, own[:slots, :].astype(jnp.float32), (((0,), (0,)), ((), ())), precision=HI,
            preferred_element_type=jnp.float32,
        )[:SEQ_ROWS]
        near = lax.dot_general(
            dense, dense, (((1,), (1,)), ((), ())), precision=HI, preferred_element_type=jnp.float32
        ) * (4.0 / math.sqrt(model_width))
        both = pairs + spans[3:4, :1] * near
        scores[...] = jnp.concatenate([both[:8], jnp.zeros((8, 128 - SEQ_ROWS), jnp.float32)], axis=1)


def logits_step(slots, at, model_width, vocab, width, bounds, pieces, ids, head, before, block, spans_own):
    columns = head.shape[1]
    n_heads = sum(p.shape[1] // width for p in pieces)
    here = pl.BlockSpec(memory_space=pltpu.VMEM)
    there = pl.BlockSpec(memory_space=pltpu.HBM)
    whole = lambda shape: vmem(shape, lambda j, s, b: (0, 0))
    tile = vmem((slots, block), lambda j, s, b: (0, j))
    first = at // width
    in_specs = [vmem(p.shape, lambda j, s, b: (0, 0), **once()) for p in pieces]
    in_specs += [vmem((width, block), (lambda i: lambda j, s, b: (s[i], j))(first + i)) for i in range(n_heads)]
    operands = list(pieces) + [head] * n_heads
    aliases = {}
    if before is not None:
        aliases = {2 + len(operands): 0, 4 + len(operands): 2}
        in_specs += [here, whole((EXTRA, width)), there]
        operands += list(before)
    out_shape = [
        pltpu.VMEM((slots, columns), jnp.float32),
        jax.ShapeDtypeStruct((EXTRA, width), jnp.float32),
        pltpu.HBM((slots, model_width), jnp.bfloat16),
    ]
    out_specs = [here, whole((EXTRA, width)), there]
    scratch = [pltpu.SemaphoreType.DMA((len(pieces),))]
    if spans_own is not None:
        per_width = -(-slots // width) * width
        in_specs += [whole(v.shape) for v in spans_own]
        operands += list(spans_own)
        table = jax.ShapeDtypeStruct((SEQ_ROWS, columns), jnp.float32)
        out_shape += [
            jax.ShapeDtypeStruct((slots, columns), jnp.float32), table, table,
            jax.ShapeDtypeStruct((8, 128), jnp.float32),
        ]
        out_specs += [tile, whole(table.shape), whole(table.shape), whole((8, 128))]
        scratch += [
            pltpu.VMEM((per_width, 128), jnp.float32),
            pltpu.VMEM((slots + WINDOW + 8, block), jnp.float32),
        ]
        kernel = functools.partial(last_kernel, slots, at, len(pieces), n_heads, model_width, vocab)
    else:
        kernel = functools.partial(partial_kernel, slots, at, len(pieces), n_heads, before is not None)
    return list(pl.pallas_call(
        kernel,
        out_shape=out_shape,
        grid_spec=pltpu.PrefetchScalarGridSpec(
            num_scalar_prefetch=2,
            grid=(columns // block,),
            in_specs=in_specs,
            out_specs=out_specs,
            scratch_shapes=scratch,
        ),
        input_output_aliases=aliases,
        compiler_params=pltpu.CompilerParams(vmem_limit_bytes=28 * MIB),
        cost_estimate=pl.CostEstimate(
            flops=2 * slots * width * n_heads * columns,
            bytes_accessed=2 * width * n_heads * columns,
            transcendentals=0,
        ),
        name="partial_logits" if spans_own is None else "last_logits",
    )(ids, bounds, *operands))


def grad_kernel(fills, vocab, ids, positive, scores, spans, total, sparse, grown, features, out, loss, glogits, mix):
    slots = features.shape[0]
    block = grown.shape[1]
    step = pl.program_id(0)

    @pl.when(step == 0)
    def _():
        row = lax.broadcasted_iota(jnp.int32, (8, 128), 0)
        lane = lax.broadcasted_iota(jnp.int32, (8, 128), 1)
        target = jnp.full((8, 128), -1, jnp.int32)
        for q in range(NQ):
            target = jnp.where(row == q, NQ + positive[q], target)
        wanted = (row < NQ) & (lane >= NQ) & (lane < NQ + NP)
        chosen = wanted & (lane == target)
        rest = wanted & (lane != target)
        value = scores[...]
        diff = value - jnp.sum(jnp.where(chosen, value, 0.0), axis=1, keepdims=True)
        softplus = jnp.maximum(diff, 0.0) + jnp.log1p(jnp.exp(-jnp.abs(diff)))
        lost = jnp.sum(jnp.where(rest, softplus, 0.0), axis=1, keepdims=True)
        loss[...] = jnp.broadcast_to(jnp.sum(lost, axis=0, keepdims=True), loss.shape)
        sig = jnp.where(rest, jax.nn.sigmoid(diff), 0.0)
        gscore = jnp.where(chosen, -jnp.sum(sig, axis=1, keepdims=True), sig)
        square = jnp.concatenate([gscore, jnp.zeros((120, 128), jnp.float32)], axis=0)
        mix[...] = (square + jnp.transpose(square))[:SEQ_ROWS]

    @pl.when(step < fills)
    def _():
        lanes = pl.ds(pl.multiple_of(step * block, block), block)
        gsparse = jnp.dot(mix[:, :SEQ_ROWS], sparse[:, lanes], precision=HI, preferred_element_type=jnp.float32)
        coef = (2.0 / math.sqrt(vocab)) * gsparse / total[:, lanes]
        parts = jnp.concatenate([*split3(coef), jnp.zeros((128 - 3 * SEQ_ROWS, block), jnp.bfloat16)], axis=0)
        member = jnp.where(members(slots, spans[...]), 1.0, 0.0).astype(jnp.bfloat16)
        glogits[:, lanes] = (dot(member, parts) * grown[...]).astype(jnp.bfloat16)

    @pl.when(step >= fills)
    def _():
        out[...] = lax.dot_general(
            features[...], glogits[...], (((0,), (0,)), ((), ())), preferred_element_type=jnp.float32
        ).astype(jnp.bfloat16)


def grad(vocab, ids, positive, scores, spans, total, sparse, grown, features, rows, block):
    slots, depth = features.shape
    columns = grown.shape[1]
    fills = columns // block
    whole = lambda v: vmem(v.shape, lambda i, s, p: (0, 0), **once())
    return pl.pallas_call(
        functools.partial(grad_kernel, fills, vocab),
        out_shape=[
            jax.ShapeDtypeStruct((depth, columns), jnp.bfloat16),
            jax.ShapeDtypeStruct((8, 128), jnp.float32),
        ],
        grid_spec=pltpu.PrefetchScalarGridSpec(
            num_scalar_prefetch=2,
            grid=(fills + depth // rows,),
            in_specs=[
                whole(scores),
                whole(spans),
                whole(total),
                whole(sparse),
                vmem((slots, block), lambda i, s, p: (0, jnp.minimum(i, fills - 1))),
                vmem((slots, rows), lambda i, s, p: (0, jnp.maximum(i - fills, 0))),
            ],
            out_specs=[
                vmem((rows, columns), lambda i, s, p: (s[jnp.maximum(i - fills, 0)], 0)),
                vmem((8, 128), lambda i, s, p: (0, 0)),
            ],
            scratch_shapes=[
                pltpu.VMEM((slots, columns), jnp.bfloat16),
                pltpu.VMEM((SEQ_ROWS, 128), jnp.float32),
            ],
        ),
        compiler_params=pltpu.CompilerParams(vmem_limit_bytes=32 * MIB),
        cost_estimate=pl.CostEstimate(
            flops=2 * slots * depth * columns,
            bytes_accessed=2 * depth * (columns + slots) + 4 * slots * columns,
            transcendentals=0,
        ),
        name="head_grad",
    )(ids, positive, scores, spans, total, sparse, grown, features)


def divisor(size, most):
    return max(b for b in range(128, most + 1, 128) if size % b == 0)


def step(slots, sizes, model_width, vocab, hidden, bounds, spans, positive, norm_gain, head):
    dp_size = sizes["dp"]
    width = hidden.shape[1]
    columns = head.shape[1]
    block = divisor(columns, 512)
    chips = dp_size // 2
    rows = chips // 2
    ring = [2 * i for i in range(rows)] + [2 * i + 1 for i in reversed(range(rows))]
    hop = []
    for i in range(chips):
        here, after, before = ring[i], ring[(i + 1) % chips], ring[(i - 1) % chips]
        hop.append((2 * here, 2 * after))
        hop.append((2 * here + 1, 2 * before + 1))
    swap = [(j, j ^ 1) for j in range(dp_size)]

    table = np.zeros((dp_size, dp_size), np.int32)
    for j in range(dp_size):
        core, here = j % 2, ring.index(j // 2)
        way = 1 - 2 * core
        got = [(here, core), (here, 1 - core)]
        for k in range(1, chips // 2):
            got += [(here - k * way, core), (here - k * way, 1 - core)]
            got += [(here + k * way, 1 - core), (here + k * way, core)]
        got += [(here + chips // 2, core), (here + chips // 2, 1 - core)]
        table[j] = [2 * ring[at % chips] + side for at, side in got]
    order = jnp.asarray(table)[lax.axis_index("dp")]

    at = 0

    def partial(pieces, before, spans_own=None):
        nonlocal at
        state = logits_step(
            slots, at, model_width, vocab, width, bounds, pieces, order, head, before, block, spans_own
        )
        at += sum(p.shape[1] for p in pieces)
        return state

    pay = pack(slots, bounds, hidden, norm_gain)
    other = lax.ppermute(pay, "dp", swap)
    held = jnp.concatenate([pay, other], axis=1)
    fresh, state = [held], None
    for _ in range(1, chips // 2):
        coming = lax.ppermute(held, "dp", hop)
        state = partial(fresh, state)
        held, state[1] = lax.optimization_barrier((coming, state[1]))
        fresh = [held, lax.ppermute(held, "dp", swap)]
    coming = lax.ppermute(held[:, :width], "dp", hop)
    state = partial(fresh, state)
    half, state[1] = lax.optimization_barrier((coming, state[1]))
    twin = lax.ppermute(half, "dp", swap)
    _, _, full, grown, total, sparse, scores = partial([half, twin], state, [spans, pay])
    scores = butterfly(scores, [("dp", dp_size), ("vocab", sizes["vocab"])])
    head_grad, loss = grad(vocab, order, positive, scores, spans, total, sparse, grown, full, width, block)
    return loss[0, 0], head_grad


def solution(mesh):
    sizes = {name: mesh.shape[name] for name in ("dp", "vocab")}

    def shards(hidden, lengths, positive, norm_gain, head):
        tokens = hidden.shape[0]
        seqs = lengths.shape[0]
        model_width = hidden.shape[1] * sizes["dp"]
        vocab = head.shape[1] * sizes["dp"] * sizes["vocab"]
        choices = [tokens * 2 // 3, tokens]
        upto = jnp.arange(seqs)[:, None] <= jnp.arange(seqs)[None, :]
        ends = jnp.sum(jnp.where(upto, lengths[:, None], 0), axis=0)
        bounds = jnp.stack([ends - lengths, ends])
        pad = lambda v: jnp.pad(v, (0, SEQ_ROWS - seqs), constant_values=0)
        leading = (lax.axis_index("vocab") == 0).astype(jnp.float32)
        lanes = [jnp.tile(pad(v.astype(jnp.float32)), 4) for v in (bounds[0], bounds[1])]
        lanes += [jnp.tile(jnp.maximum(pad(lengths), 1).astype(jnp.float32), 4), jnp.full((128,), leading)]
        spans = jnp.pad(jnp.stack(lanes), ((0, 4), (0, 0)))
        which = sum((ends[-1] > t).astype(jnp.int32) for t in choices[:-1])
        branches = [
            (lambda t: lambda *a: step(t, sizes, model_width, vocab, *a))(t) for t in choices
        ]
        return lax.switch(which, branches, hidden, bounds, spans, positive, norm_gain, head)

    in_specs = (P(None, "dp"), P(), P(), P("dp"), P(None, ("dp", "vocab")))
    out_specs = (P(), P(None, ("dp", "vocab")))
    return jax.shard_map(shards, mesh=mesh, in_specs=in_specs, out_specs=out_specs, check_vma=False)
```

```python
import functools
import math

import jax
import jax.numpy as jnp
import numpy as np
from jax import lax
from jax.experimental import pallas as pl
from jax.experimental.pallas import tpu as pltpu
from jax.sharding import PartitionSpec as P

SEQ = 32
NQ = 4
NP = 20
SEQ_ROWS = 32
EXTRA = 16
WINDOW = SEQ + 8
HI = lax.Precision.HIGHEST
MIB = 1024 * 1024


def split3(x):
    a = x.astype(jnp.bfloat16)
    rest = x - a.astype(jnp.float32)
    b = rest.astype(jnp.bfloat16)
    c = (rest - b.astype(jnp.float32)).astype(jnp.bfloat16)
    return a, b, c


def dot(a, b):
    return jnp.dot(a, b, preferred_element_type=jnp.float32)


def vmem(shape, index, **kw):
    return pl.BlockSpec(shape, index, **kw)


def once():
    return dict(pipeline_mode=pl.Buffered(1))


def starts_of(lengths):
    start, spans = 0, []
    for s in range(lengths.shape[0]):
        spans.append((start, lengths[s]))
        start = start + lengths[s]
    return spans


def pack_kernel(slots, lengths, hidden, gain, pay, spans):
    tokens, width = hidden.shape
    per = -(-slots // width)
    token = lax.broadcasted_iota(jnp.int32, (8, tokens), 1)
    seq, place = token // SEQ, token % SEQ
    row, lane = lax.broadcasted_iota(jnp.int32, (8, 128), 0), lax.broadcasted_iota(jnp.int32, (8, 128), 1)
    target = jnp.full((8, tokens), -1, jnp.int32)
    table = jnp.where(row == 2, 1, 0)
    for s, (start, length) in enumerate(starts_of(lengths)):
        target = jnp.where((seq == s) & (place < length), start + place, target)
        mine = lane % SEQ_ROWS == s
        for r, value in enumerate((start, start + length, length)):
            table = jnp.where(mine & (row == r), value, table)
    spans[...] = table.astype(jnp.float32)
    slot = lax.broadcasted_iota(jnp.int32, (slots, tokens), 0)
    pick = jnp.where(slot == target[:1], 1.0, 0.0).astype(jnp.bfloat16)
    packed = dot(pick, hidden[...])
    pay[:slots, :] = (packed * gain[...].astype(jnp.float32).reshape(1, width)).astype(jnp.bfloat16)
    terms = split3(packed * packed)[:2]
    squares = sum(
        lax.dot_general(
            jnp.ones((16, width), jnp.bfloat16), term, (((1,), (1,)), ((), ())), preferred_element_type=jnp.float32
        )
        for term in terms
    )
    row = lax.broadcasted_iota(jnp.int32, (EXTRA, width), 0)
    extra = jnp.zeros((EXTRA, width), jnp.float32)
    for q in range(per):
        lanes = squares[:1, q * width : min((q + 1) * width, slots)]
        if lanes.shape[1] < width:
            lanes = jnp.concatenate([lanes, jnp.zeros((1, width - lanes.shape[1]), jnp.float32)], axis=1)
        for i, v in enumerate(split3(lanes)):
            extra = jnp.where(row == 3 * q + i, v.astype(jnp.float32), extra)
    pay[slots:, :] = extra.astype(jnp.bfloat16)


def pack(slots, lengths, hidden, gain):
    tokens, width = hidden.shape
    return pl.pallas_call(
        functools.partial(pack_kernel, slots),
        out_shape=[
            jax.ShapeDtypeStruct((slots + EXTRA, width), jnp.bfloat16),
            jax.ShapeDtypeStruct((8, 128), jnp.float32),
        ],
        grid_spec=pltpu.PrefetchScalarGridSpec(
            num_scalar_prefetch=1,
            grid=(1,),
            in_specs=[
                vmem((tokens, width), lambda i, b: (0, 0)),
                vmem((width,), lambda i, b: (0,)),
            ],
            out_specs=[
                vmem((slots + EXTRA, width), lambda i, b: (0, 0)),
                vmem((8, 128), lambda i, b: (0, 0)),
            ],
        ),
        compiler_params=pltpu.CompilerParams(vmem_limit_bytes=32 * MIB),
        cost_estimate=pl.CostEstimate(
            flops=2 * slots * tokens * width, bytes_accessed=2 * (tokens + slots) * width, transcendentals=0
        ),
        name="pack",
    )(lengths, hidden, gain)


def take(slots, at, pieces, heads, acc, sums_in, sums, kept, sem):
    width = heads[0].shape[0]
    copies = []
    for piece in pieces:
        copies.append(
            pltpu.make_async_copy(piece.at[:slots, :], kept.at[:, pl.ds(at, piece.shape[1])], sem.at[len(copies)])
        )
        at += piece.shape[1]

    @pl.when(pl.program_id(0) == 0)
    def _():
        for copy in copies:
            copy.start()
        extra = jnp.zeros(sums.shape, jnp.float32) if sums_in is None else sums_in[...]
        for piece in pieces:
            for h in range(piece.shape[1] // width):
                extra = extra + piece[slots:, h * width : (h + 1) * width].astype(jnp.float32)
        sums[...] = extra

    left = [piece[:slots, :] for piece in pieces]
    left = left[0] if len(left) == 1 else jnp.concatenate(left, axis=1)
    part = dot(left, jnp.concatenate([head[...] for head in heads], axis=0))
    acc = part if acc is None else acc + part

    @pl.when(pl.program_id(0) == pl.num_programs(0) - 1)
    def _():
        for copy in copies:
            copy.wait()

    return acc


def lanes_of(block):
    return pl.ds(pl.multiple_of(pl.program_id(0) * block, block), block)


def partial_kernel(slots, at, n_pieces, n_heads, has_before, ids, lengths, *refs):
    pieces, refs = refs[:n_pieces], refs[n_pieces:]
    heads, refs = refs[:n_heads], refs[n_heads:]
    acc_in, sums_in, _, acc, sums, kept, sem = refs if has_before else (None, None, None, *refs)
    lanes = lanes_of(heads[0].shape[1])
    before = acc_in[:, lanes] if has_before else None
    acc[:, lanes] = take(slots, at, pieces, heads, before, sums_in, sums, kept, sem)


def members(slots, spans):
    slot = lax.broadcasted_iota(jnp.int32, (slots, 128), 0).astype(jnp.float32)
    return (slot >= spans[0:1, :]) & (slot < spans[1:2, :])


def last_kernel(slots, at, n_pieces, n_heads, model_width, vocab, copies, ids, lengths, *refs):
    pieces, refs = refs[:n_pieces], refs[n_pieces:]
    heads, refs = refs[:n_heads], refs[n_heads:]
    acc_in, sums_in, kept_in, spans, grown, sums, kept, total, sparse, scores, sem, scale, expo, folded, own, own_sem = refs
    width, block = heads[0].shape
    per = -(-slots // width)
    lanes = lanes_of(block)
    first, final = pl.program_id(0) == 0, pl.program_id(0) == pl.num_programs(0) - 1
    fetch = pltpu.make_async_copy(kept_in.at[:, pl.ds(0, width)], own, own_sem)

    @pl.when(first)
    def _():
        fetch.start()

    x = take(slots, at, pieces, heads, acc_in[:, lanes], sums_in, sums, kept, sem)

    @pl.when(first)
    def _():
        rows = [sums[3 * q : 3 * q + 1] + sums[3 * q + 1 : 3 * q + 2] + sums[3 * q + 2 : 3 * q + 3] for q in range(per)]
        line = jnp.concatenate(rows, axis=1) if per > 1 else rows[0]
        line = lax.rsqrt(line / model_width + 1e-05)
        scale[...] = jnp.transpose(jnp.broadcast_to(line, (128, per * width)))
        total[...] = jnp.ones(total.shape, jnp.float32)

    by = scale[:slots, :]
    for i in range(block // 128):
        part = slice(i * 128, (i + 1) * 128)
        ramp = jnp.maximum(x[:, part] * by, 0.0)
        one = 1.0 + ramp * ramp
        two = one * one
        expo[:slots, part] = two * two
        grown[:, pl.ds(pl.multiple_of(pl.program_id(0) * block + i * 128, 128), 128)] = ramp * one * two * by

    for s, (start, length) in enumerate(starts_of(lengths)):
        base = pl.multiple_of((start // 8) * 8, 8)
        row = base + lax.broadcasted_iota(jnp.int32, (WINDOW, 128), 0)
        inside = (row >= start) & (row < start + length)
        for i in range(block // 128):
            part = slice(i * 128, (i + 1) * 128)
            values = jnp.where(inside, expo[pl.ds(base, WINDOW), part], 0.0)
            folded[i, 8 * s : 8 * s + 8, :] = jnp.sum(values.reshape(WINDOW // 8, 8, 128), axis=0)
    seqs = lengths.shape[0]
    for i in range(block // 128):
        part = pl.ds(pl.multiple_of(pl.program_id(0) * block + i * 128, 128), 128)
        total[:seqs, part] = sum(folded[i, pl.ds(j, seqs, stride=8), :] for j in range(8))

    @pl.when(final)
    def _():
        counts = jnp.transpose(jnp.broadcast_to(spans[2:3, :], (128, 128)))[:SEQ_ROWS]

        @pl.loop(0, total.shape[1] // 128)
        def _(i):
            part = pl.ds(pl.multiple_of(i * 128, 128), 128)
            sparse[:, part] = 0.25 * jnp.log(total[:, part] / counts)

        pairs = lax.dot_general(
            sparse[...], sparse[...], (((1,), (1,)), ((), ())), precision=HI, preferred_element_type=jnp.float32
        ) / math.sqrt(vocab)
        fetch.wait()
        weight = jnp.where(members(slots, spans[...]), by / spans[2:3, :], 0.0)
        high, mid, low = split3(weight)
        third = lax.broadcasted_iota(jnp.int32, weight.shape, 1) // SEQ_ROWS
        weight = jnp.where(third == 0, high.astype(jnp.float32), jnp.where(third == 1, mid.astype(jnp.float32), low.astype(jnp.float32)))
        dense = lax.dot_general(
            weight.astype(jnp.bfloat16), own[...], (((0,), (0,)), ((), ())), preferred_element_type=jnp.float32
        )
        dense = dense[:SEQ_ROWS] + dense[SEQ_ROWS : 2 * SEQ_ROWS] + dense[2 * SEQ_ROWS : 3 * SEQ_ROWS]
        near = lax.dot_general(
            dense, dense, (((1,), (1,)), ((), ())), precision=HI, preferred_element_type=jnp.float32
        ) * (4.0 / (math.sqrt(model_width) * copies))
        both = pairs + near
        tile = jnp.concatenate([both[:8], jnp.zeros((8, 128 - SEQ_ROWS), jnp.float32)], axis=1)

        @pl.loop(0, scores.shape[0] // 8)
        def _(i):
            scores[pl.ds(pl.multiple_of(8 * i, 8), 8), :] = tile


def logits_step(slots, at, model_width, vocab, copies, devices, width, lengths, pieces, ids, head, before, block, spans):
    columns = head.shape[1]
    n_heads = sum(p.shape[1] // width for p in pieces)
    here = pl.BlockSpec(memory_space=pltpu.VMEM)
    there = pl.BlockSpec(memory_space=pltpu.HBM)
    whole = lambda shape: vmem(shape, lambda j, s, b: (0, 0))
    first = at // width
    in_specs = [vmem(p.shape, lambda j, s, b: (0, 0), **once()) for p in pieces]
    in_specs += [vmem((width, block), (lambda i: lambda j, s, b: (s[i], j))(first + i)) for i in range(n_heads)]
    operands = list(pieces) + [head] * n_heads
    aliases = {}
    if before is not None:
        aliases = {2 + len(operands): 0, 4 + len(operands): 2}
        in_specs += [here, whole((EXTRA, width)), there]
        operands += list(before)
    out_shape = [
        pltpu.VMEM((slots, columns), jnp.float32),
        jax.ShapeDtypeStruct((EXTRA, width), jnp.float32),
        pltpu.HBM((slots, model_width), jnp.bfloat16),
    ]
    out_specs = [here, whole((EXTRA, width)), there]
    scratch = [pltpu.SemaphoreType.DMA((len(pieces),))]
    if spans is not None:
        per_width = -(-slots // width) * width
        in_specs.append(whole(spans.shape))
        operands.append(spans)
        table = jax.ShapeDtypeStruct((SEQ_ROWS, columns), jnp.float32)
        out_shape += [
            table, table, jax.ShapeDtypeStruct((8 * devices, 128), jnp.float32),
        ]
        out_specs += [whole(table.shape), whole(table.shape), whole((8 * devices, 128))]
        scratch += [
            pltpu.VMEM((per_width, 128), jnp.float32),
            pltpu.VMEM((slots + WINDOW + 8, block), jnp.float32),
            pltpu.VMEM((block // 128, 8 * lengths.shape[0], 128), jnp.float32),
            pltpu.VMEM((slots, width), jnp.bfloat16),
            pltpu.SemaphoreType.DMA(()),
        ]
        kernel = functools.partial(last_kernel, slots, at, len(pieces), n_heads, model_width, vocab, copies)
    else:
        kernel = functools.partial(partial_kernel, slots, at, len(pieces), n_heads, before is not None)
    return list(pl.pallas_call(
        kernel,
        out_shape=out_shape,
        grid_spec=pltpu.PrefetchScalarGridSpec(
            num_scalar_prefetch=2,
            grid=(columns // block,),
            in_specs=in_specs,
            out_specs=out_specs,
            scratch_shapes=scratch,
        ),
        input_output_aliases=aliases,
        compiler_params=pltpu.CompilerParams(vmem_limit_bytes=28 * MIB),
        cost_estimate=pl.CostEstimate(
            flops=2 * slots * width * n_heads * columns,
            bytes_accessed=2 * width * n_heads * columns,
            transcendentals=0,
        ),
        name="partial_logits" if spans is None else "last_logits",
    )(ids, lengths, *operands))


def grad_kernel(fill, vocab, ids, positive, scores, spans, total, sparse, grown, features, out, loss, glogits, mix):
    slots = features.shape[0]
    step = pl.program_id(0)

    @pl.when(step == 0)
    def _():
        row = lax.broadcasted_iota(jnp.int32, (8, 128), 0)
        lane = lax.broadcasted_iota(jnp.int32, (8, 128), 1)
        target = jnp.full((8, 128), -1, jnp.int32)
        for q in range(NQ):
            target = jnp.where(row == q, NQ + positive[q], target)
        wanted = (row < NQ) & (lane >= NQ) & (lane < NQ + NP)
        chosen = wanted & (lane == target)
        rest = wanted & (lane != target)
        value = jnp.sum(scores[...].reshape(scores.shape[0] // 8, 8, 128), axis=0)
        diff = value - jnp.sum(jnp.where(chosen, value, 0.0), axis=1, keepdims=True)
        softplus = jnp.maximum(diff, 0.0) + jnp.log1p(jnp.exp(-jnp.abs(diff)))
        lost = jnp.sum(jnp.where(rest, softplus, 0.0), axis=1, keepdims=True)
        loss[0, 0] = jnp.sum(lost)
        sig = jnp.where(rest, jax.nn.sigmoid(diff), 0.0)
        gscore = jnp.where(chosen, -jnp.sum(sig, axis=1, keepdims=True), sig)
        square = jnp.concatenate([gscore, jnp.zeros((120, 128), jnp.float32)], axis=0)
        mix[...] = (square + jnp.transpose(square))[:SEQ_ROWS]

        member = jnp.where(members(slots, spans[...]), 1.0, 0.0).astype(jnp.bfloat16)

        @pl.loop(0, grown.shape[1] // fill)
        def _(j):
            lanes = pl.ds(pl.multiple_of(j * fill, fill), fill)
            gsparse = jnp.dot(mix[:, :SEQ_ROWS], sparse[:, lanes], precision=HI, preferred_element_type=jnp.float32)
            coef = (2.0 / math.sqrt(vocab)) * gsparse / total[:, lanes]
            parts = jnp.concatenate([*split3(coef), jnp.zeros((128 - 3 * SEQ_ROWS, fill), jnp.bfloat16)], axis=0)
            glogits[:, lanes] = (dot(member, parts) * grown[:, lanes]).astype(jnp.bfloat16)

    out[...] = lax.dot_general(
        features[...], glogits[...], (((0,), (0,)), ((), ())), preferred_element_type=jnp.float32
    ).astype(jnp.bfloat16)


def grad(vocab, ids, positive, scores, spans, total, sparse, grown, features, rows, block):
    slots, depth = features.shape
    columns = grown.shape[1]
    fill = divisor(columns, 2 * block)
    whole = lambda v: vmem(v.shape, lambda i, s, p: (0, 0), **once())
    return pl.pallas_call(
        functools.partial(grad_kernel, fill, vocab),
        out_shape=[
            jax.ShapeDtypeStruct((depth, columns), jnp.bfloat16),
            jax.ShapeDtypeStruct((1, 1), jnp.float32),
        ],
        grid_spec=pltpu.PrefetchScalarGridSpec(
            num_scalar_prefetch=2,
            grid=(depth // rows,),
            in_specs=[
                whole(scores),
                whole(spans),
                whole(total),
                whole(sparse),
                pl.BlockSpec(memory_space=pltpu.VMEM),
                vmem((slots, rows), lambda i, s, p: (0, i)),
            ],
            out_specs=[
                vmem((rows, columns), lambda i, s, p: (s[i], 0)),
                pl.BlockSpec(memory_space=pltpu.SMEM),
            ],
            scratch_shapes=[
                pltpu.VMEM((slots, columns), jnp.bfloat16),
                pltpu.VMEM((SEQ_ROWS, 128), jnp.float32),
            ],
        ),
        compiler_params=pltpu.CompilerParams(vmem_limit_bytes=40 * MIB),
        cost_estimate=pl.CostEstimate(
            flops=2 * slots * depth * columns,
            bytes_accessed=2 * depth * (columns + slots) + 4 * slots * columns,
            transcendentals=0,
        ),
        name="head_grad",
    )(ids, positive, scores, spans, total, sparse, grown, features)


def divisor(size, most):
    return max(b for b in range(128, most + 1, 128) if size % b == 0)


def step(slots, sizes, model_width, vocab, hidden, lengths, positive, norm_gain, head):
    dp_size = sizes["dp"]
    devices = dp_size * sizes["vocab"]
    width = hidden.shape[1]
    columns = head.shape[1]
    block = divisor(columns, 512 if 4 * slots <= 3 * SEQ * lengths.shape[0] else 256)
    chips = dp_size // 2
    rows = chips // 2
    ring = [2 * i for i in range(rows)] + [2 * i + 1 for i in reversed(range(rows))]
    hop = []
    for i in range(chips):
        here, after, before = ring[i], ring[(i + 1) % chips], ring[(i - 1) % chips]
        hop.append((2 * here, 2 * after))
        hop.append((2 * here + 1, 2 * before + 1))
    swap = [(j, j ^ 1) for j in range(dp_size)]

    table = np.zeros((dp_size, dp_size), np.int32)
    for j in range(dp_size):
        core, here = j % 2, ring.index(j // 2)
        way = 1 - 2 * core
        got = [(here, core), (here, 1 - core)]
        for k in range(1, chips // 2):
            got += [(here - k * way, core), (here - k * way, 1 - core)]
            got += [(here + k * way, 1 - core), (here + k * way, core)]
        got += [(here + chips // 2, core), (here + chips // 2, 1 - core)]
        table[j] = [2 * ring[at % chips] + side for at, side in got]
    order = jnp.asarray(table)[lax.axis_index("dp")]

    at = 0

    def partial(pieces, before, spans=None):
        nonlocal at
        state = logits_step(
            slots, at, model_width, vocab, sizes["vocab"], devices, width, lengths, pieces, order, head, before,
            block, spans,
        )
        at += sum(p.shape[1] for p in pieces)
        return state

    pay, spans = pack(slots, lengths, hidden, norm_gain)
    other = lax.ppermute(pay, "dp", swap)
    held = jnp.concatenate([pay, other], axis=1)
    fresh, state = [held], None
    for _ in range(1, chips // 2):
        coming = lax.ppermute(held, "dp", hop)
        state = partial(fresh, state)
        held, state[1] = lax.optimization_barrier((coming, state[1]))
        fresh = [held, lax.ppermute(held, "dp", swap)]
    coming = lax.ppermute(held[:, :width], "dp", hop)
    state = partial(fresh, state)
    half, state[1] = lax.optimization_barrier((coming, state[1]))
    twin = lax.ppermute(half, "dp", swap)
    grown, _, full, total, sparse, scores = partial([half, twin], state, spans)
    scores = lax.all_to_all(scores, ("dp", "vocab"), 0, 0, tiled=True)
    head_grad, loss = grad(vocab, order, positive, scores, spans, total, sparse, grown, full, width, block)
    return loss[0, 0], head_grad


def solution(mesh):
    sizes = {name: mesh.shape[name] for name in ("dp", "vocab")}

    def shards(hidden, lengths, positive, norm_gain, head):
        tokens = hidden.shape[0]
        model_width = hidden.shape[1] * sizes["dp"]
        vocab = head.shape[1] * sizes["dp"] * sizes["vocab"]
        choices = [tokens * 2 // 3, tokens * 3 // 4, tokens]
        used = jnp.sum(lengths)
        which = sum((used > t).astype(jnp.int32) for t in choices[:-1])
        branches = [
            (lambda t: lambda *a: step(t, sizes, model_width, vocab, *a))(t) for t in choices
        ]
        return lax.switch(which, branches, hidden, lengths, positive, norm_gain, head)

    in_specs = (P(None, "dp"), P(), P(), P("dp"), P(None, ("dp", "vocab")))
    out_specs = (P(), P(None, ("dp", "vocab")))
    return jax.shard_map(shards, mesh=mesh, in_specs=in_specs, out_specs=out_specs, check_vma=False)
```

```python
import functools
import math

import jax
import jax.numpy as jnp
import numpy as np
from jax import lax
from jax.experimental import pallas as pl
from jax.experimental.pallas import tpu as pltpu
from jax.sharding import PartitionSpec as P

SEQ = 32
NQ = 4
NP = 20
SEQ_ROWS = 32
EXTRA = 16
HI = lax.Precision.HIGHEST
MIB = 1024 * 1024


def split3(x):
    a = x.astype(jnp.bfloat16)
    rest = x - a.astype(jnp.float32)
    b = rest.astype(jnp.bfloat16)
    c = (rest - b.astype(jnp.float32)).astype(jnp.bfloat16)
    return a, b, c


def dot(a, b):
    return jnp.dot(a, b, preferred_element_type=jnp.float32)


def vmem(shape, index, **kw):
    return pl.BlockSpec(shape, index, **kw)


def once():
    return dict(pipeline_mode=pl.Buffered(1))


def starts_of(lengths):
    start, spans = 0, []
    for s in range(lengths.shape[0]):
        spans.append((start, lengths[s]))
        start = start + lengths[s]
    return spans


def pack_kernel(slots, lengths, hidden, gain, pay, spans):
    tokens, width = hidden.shape
    per = -(-slots // width)
    token = lax.broadcasted_iota(jnp.int32, (8, tokens), 1)
    seq, place = token // SEQ, token % SEQ
    row, lane = lax.broadcasted_iota(jnp.int32, (8, 128), 0), lax.broadcasted_iota(jnp.int32, (8, 128), 1)
    target = jnp.full((8, tokens), -1, jnp.int32)
    table = jnp.where(row == 2, 1, 0)
    for s, (start, length) in enumerate(starts_of(lengths)):
        target = jnp.where((seq == s) & (place < length), start + place, target)
        mine = lane % SEQ_ROWS == s
        for r, value in enumerate((start, start + length, length)):
            table = jnp.where(mine & (row == r), value, table)
    spans[...] = table.astype(jnp.float32)
    slot = lax.broadcasted_iota(jnp.int32, (slots, tokens), 0)
    pick = jnp.where(slot == target[:1], 1.0, 0.0).astype(jnp.bfloat16)
    packed = dot(pick, hidden[...])
    pay[:slots, :] = (packed * gain[...].astype(jnp.float32).reshape(1, width)).astype(jnp.bfloat16)
    terms = split3(packed * packed)[:2]
    squares = sum(
        lax.dot_general(
            jnp.ones((16, width), jnp.bfloat16), term, (((1,), (1,)), ((), ())), preferred_element_type=jnp.float32
        )
        for term in terms
    )
    row = lax.broadcasted_iota(jnp.int32, (EXTRA, width), 0)
    extra = jnp.zeros((EXTRA, width), jnp.float32)
    for q in range(per):
        lanes = squares[:1, q * width : min((q + 1) * width, slots)]
        if lanes.shape[1] < width:
            lanes = jnp.concatenate([lanes, jnp.zeros((1, width - lanes.shape[1]), jnp.float32)], axis=1)
        for i, v in enumerate(split3(lanes)):
            extra = jnp.where(row == 3 * q + i, v.astype(jnp.float32), extra)
    pay[slots:, :] = extra.astype(jnp.bfloat16)


def pack(slots, lengths, hidden, gain):
    tokens, width = hidden.shape
    return pl.pallas_call(
        functools.partial(pack_kernel, slots),
        out_shape=[
            jax.ShapeDtypeStruct((slots + EXTRA, width), jnp.bfloat16),
            jax.ShapeDtypeStruct((8, 128), jnp.float32),
        ],
        grid_spec=pltpu.PrefetchScalarGridSpec(
            num_scalar_prefetch=1,
            grid=(1,),
            in_specs=[
                vmem((tokens, width), lambda i, b: (0, 0)),
                vmem((width,), lambda i, b: (0,)),
            ],
            out_specs=[
                vmem((slots + EXTRA, width), lambda i, b: (0, 0)),
                vmem((8, 128), lambda i, b: (0, 0)),
            ],
        ),
        compiler_params=pltpu.CompilerParams(vmem_limit_bytes=32 * MIB),
        cost_estimate=pl.CostEstimate(
            flops=2 * slots * tokens * width, bytes_accessed=2 * (tokens + slots) * width, transcendentals=0
        ),
        name="pack",
    )(lengths, hidden, gain)


def take(slots, at, pieces, heads, acc, sums_in, sums, kept, sem):
    width = heads[0].shape[0]
    copies, left, behind = [], [], []
    for piece in pieces:
        row, values = 0, []
        for part in piece:
            rows = min(part.shape[0], slots - row)
            copies.append(
                pltpu.make_async_copy(
                    part.at[:rows, :], kept.at[pl.ds(row, rows), pl.ds(at, width)], sem.at[len(copies)]
                )
            )
            values.append(part[:rows, :])
            row += rows
        left.append(values[0] if len(values) == 1 else jnp.concatenate(values, axis=0))
        behind.append((piece[-1], rows))
        at += width

    @pl.when(pl.program_id(0) == 0)
    def _():
        for copy in copies:
            copy.start()
        extra = jnp.zeros(sums.shape, jnp.float32) if sums_in is None else sums_in[...]
        for part, rows in behind:
            extra = extra + part[rows:, :].astype(jnp.float32)
        sums[...] = extra

    part = dot(jnp.concatenate(left, axis=1), jnp.concatenate([head[...] for head in heads], axis=0))
    acc = part if acc is None else acc + part

    @pl.when(pl.program_id(0) == pl.num_programs(0) - 1)
    def _():
        for copy in copies:
            copy.wait()

    return acc


def grouped(refs, parts):
    n = sum(parts)
    ends = [sum(parts[: i + 1]) for i in range(len(parts))]
    pieces = [refs[end - size : end] for end, size in zip(ends, parts)]
    return pieces, refs[n : n + len(parts)], refs[n + len(parts) :]


def lanes_of(block):
    return pl.ds(pl.multiple_of(pl.program_id(0) * block, block), block)


def partial_kernel(slots, at, parts, has_before, ids, lengths, *refs):
    pieces, heads, refs = grouped(refs, parts)
    acc_in, sums_in, _, acc, sums, kept, sem = refs if has_before else (None, None, None, *refs)
    lanes = lanes_of(heads[0].shape[1])
    before = acc_in[:, lanes] if has_before else None
    acc[:, lanes] = take(slots, at, pieces, heads, before, sums_in, sums, kept, sem)


def members(slots, spans):
    slot = lax.broadcasted_iota(jnp.int32, (slots, 128), 0).astype(jnp.float32)
    return (slot >= spans[0:1, :]) & (slot < spans[1:2, :])


def last_kernel(slots, at, parts, model_width, vocab, copies, ids, lengths, *refs):
    pieces, heads, refs = grouped(refs, parts)
    acc_in, sums_in, kept_in, spans, grown, sums, kept, total, sparse, scores, sem, scale, joined, counts, own, own_sem = refs
    width, block = heads[0].shape
    per = -(-slots // width)
    lanes = lanes_of(block)
    first, final = pl.program_id(0) == 0, pl.program_id(0) == pl.num_programs(0) - 1
    fetch = pltpu.make_async_copy(kept_in.at[:, pl.ds(0, width)], own, own_sem)

    @pl.when(first)
    def _():
        fetch.start()

    x = take(slots, at, pieces, heads, acc_in[:, lanes], sums_in, sums, kept, sem)

    @pl.when(first)
    def _():
        rows = [sums[3 * q : 3 * q + 1] + sums[3 * q + 1 : 3 * q + 2] + sums[3 * q + 2 : 3 * q + 3] for q in range(per)]
        line = jnp.concatenate(rows, axis=1) if per > 1 else rows[0]
        line = lax.rsqrt(line / model_width + 1e-05)
        scale[...] = jnp.transpose(jnp.broadcast_to(line, (128, per * width)))
        counts[...] = jnp.transpose(jnp.broadcast_to(spans[2:3, :], (128, 128)))[:SEQ_ROWS]
        member = jnp.where(members(slots, spans[...]), 1.0, 0.0)
        joined[...] = jnp.transpose(member)[:SEQ_ROWS].astype(jnp.bfloat16)

    by = scale[:slots, :]
    seqs = lengths.shape[0]
    terms = []
    for i in range(block // 128):
        part = pl.ds(pl.multiple_of(pl.program_id(0) * block + i * 128, 128), 128)
        ramp = jnp.maximum(x[:, i * 128 : (i + 1) * 128] * by, 0.0)
        one = 1.0 + ramp * ramp
        two = one * one
        grown[:, part] = ramp * one * two * by
        terms.append(split3(two * two)[:2])
    summed = sum(dot(joined[...], jnp.concatenate(term, axis=1)) for term in zip(*terms))
    summed = jnp.where(lax.broadcasted_iota(jnp.int32, summed.shape, 0) < seqs, summed, 1.0)
    total[:, lanes] = summed
    sparse[:, lanes] = 0.25 * jnp.log(summed / jnp.concatenate([counts[...]] * (block // 128), axis=1))

    @pl.when(final)
    def _():
        terms = jnp.concatenate([*split3(sparse[...]), jnp.zeros((128 - 3 * SEQ_ROWS, sparse.shape[1]), jnp.bfloat16)], axis=0)
        pairs = lax.dot_general(terms, terms, (((1,), (1,)), ((), ())), preferred_element_type=jnp.float32)
        pairs = pairs[:SEQ_ROWS] + pairs[SEQ_ROWS : 2 * SEQ_ROWS] + pairs[2 * SEQ_ROWS : 3 * SEQ_ROWS]
        pairs = pairs + pltpu.roll(pairs, 128 - SEQ_ROWS, 1) + pltpu.roll(pairs, 128 - 2 * SEQ_ROWS, 1)
        pairs = pairs / math.sqrt(vocab)
        fetch.wait()
        weight = jnp.where(members(slots, spans[...]), by / spans[2:3, :], 0.0)
        high, mid, low = split3(weight)
        third = lax.broadcasted_iota(jnp.int32, weight.shape, 1) // SEQ_ROWS
        weight = jnp.where(third == 0, high.astype(jnp.float32), jnp.where(third == 1, mid.astype(jnp.float32), low.astype(jnp.float32)))
        dense = lax.dot_general(
            weight.astype(jnp.bfloat16), own[...], (((0,), (0,)), ((), ())), preferred_element_type=jnp.float32
        )
        dense = dense[:SEQ_ROWS] + dense[SEQ_ROWS : 2 * SEQ_ROWS] + dense[2 * SEQ_ROWS : 3 * SEQ_ROWS]
        near = lax.dot_general(
            dense, jnp.concatenate([dense] * 4, axis=0), (((1,), (1,)), ((), ())), precision=HI,
            preferred_element_type=jnp.float32,
        ) * (4.0 / (math.sqrt(model_width) * copies))
        tile = (pairs + near)[:8]

        @pl.loop(0, scores.shape[0] // 8)
        def _(i):
            scores[pl.ds(pl.multiple_of(8 * i, 8), 8), :] = tile


def logits_step(slots, at, model_width, vocab, copies, devices, width, lengths, pieces, ids, head, before, block, spans):
    columns = head.shape[1]
    parts = tuple(len(piece) for piece in pieces)
    arrays = [part for piece in pieces for part in piece]
    n_heads = len(pieces)
    here = pl.BlockSpec(memory_space=pltpu.VMEM)
    there = pl.BlockSpec(memory_space=pltpu.HBM)
    whole = lambda shape: vmem(shape, lambda j, s, b: (0, 0))
    first = at // width
    in_specs = [vmem(p.shape, lambda j, s, b: (0, 0), **once()) for p in arrays]
    in_specs += [vmem((width, block), (lambda i: lambda j, s, b: (s[i], j))(first + i)) for i in range(n_heads)]
    operands = arrays + [head] * n_heads
    aliases = {}
    if before is not None:
        aliases = {2 + len(operands): 0, 4 + len(operands): 2}
        in_specs += [here, whole((EXTRA, width)), there]
        operands += list(before)
    out_shape = [
        pltpu.VMEM((slots, columns), jnp.float32),
        jax.ShapeDtypeStruct((EXTRA, width), jnp.float32),
        pltpu.HBM((slots, model_width), jnp.bfloat16),
    ]
    out_specs = [here, whole((EXTRA, width)), there]
    scratch = [pltpu.SemaphoreType.DMA((len(arrays),))]
    if spans is not None:
        per_width = -(-slots // width) * width
        in_specs.append(whole(spans.shape))
        operands.append(spans)
        table = jax.ShapeDtypeStruct((SEQ_ROWS, columns), jnp.float32)
        out_shape += [
            table, table, jax.ShapeDtypeStruct((8 * devices, 128), jnp.float32),
        ]
        out_specs += [whole(table.shape), whole(table.shape), whole((8 * devices, 128))]
        scratch += [
            pltpu.VMEM((per_width, 128), jnp.float32),
            pltpu.VMEM((SEQ_ROWS, slots), jnp.bfloat16),
            pltpu.VMEM((SEQ_ROWS, 128), jnp.float32),
            pltpu.VMEM((slots, width), jnp.bfloat16),
            pltpu.SemaphoreType.DMA(()),
        ]
        kernel = functools.partial(last_kernel, slots, at, parts, model_width, vocab, copies)
    else:
        kernel = functools.partial(partial_kernel, slots, at, parts, before is not None)
    return list(pl.pallas_call(
        kernel,
        out_shape=out_shape,
        grid_spec=pltpu.PrefetchScalarGridSpec(
            num_scalar_prefetch=2,
            grid=(columns // block,),
            in_specs=in_specs,
            out_specs=out_specs,
            scratch_shapes=scratch,
        ),
        input_output_aliases=aliases,
        compiler_params=pltpu.CompilerParams(vmem_limit_bytes=28 * MIB),
        cost_estimate=pl.CostEstimate(
            flops=2 * slots * width * n_heads * columns,
            bytes_accessed=2 * width * n_heads * columns,
            transcendentals=0,
        ),
        name="partial_logits" if spans is None else "last_logits",
    )(ids, lengths, *operands))


def grad_kernel(fill, vocab, ids, positive, scores, spans, total, sparse, grown, features, out, loss, glogits, mix):
    slots = features.shape[0]
    step = pl.program_id(0)

    @pl.when(step == 0)
    def _():
        row = lax.broadcasted_iota(jnp.int32, (8, 128), 0)
        lane = lax.broadcasted_iota(jnp.int32, (8, 128), 1)
        target = jnp.full((8, 128), -1, jnp.int32)
        for q in range(NQ):
            target = jnp.where(row == q, NQ + positive[q], target)
        wanted = (row < NQ) & (lane >= NQ) & (lane < NQ + NP)
        chosen = wanted & (lane == target)
        rest = wanted & (lane != target)
        value = jnp.sum(scores[...].reshape(scores.shape[0] // 8, 8, 128), axis=0)
        diff = value - jnp.sum(jnp.where(chosen, value, 0.0), axis=1, keepdims=True)
        softplus = jnp.maximum(diff, 0.0) + jnp.log1p(jnp.exp(-jnp.abs(diff)))
        lost = jnp.sum(jnp.where(rest, softplus, 0.0), axis=1, keepdims=True)
        loss[0, 0] = jnp.sum(lost)
        sig = jnp.where(rest, jax.nn.sigmoid(diff), 0.0)
        gscore = jnp.where(chosen, -jnp.sum(sig, axis=1, keepdims=True), sig)
        square = jnp.concatenate([gscore, jnp.zeros((120, 128), jnp.float32)], axis=0)
        mix[...] = (square + jnp.transpose(square))[:SEQ_ROWS]

        member = jnp.where(members(slots, spans[...]), 1.0, 0.0).astype(jnp.bfloat16)

        @pl.loop(0, grown.shape[1] // fill)
        def _(j):
            lanes = pl.ds(pl.multiple_of(j * fill, fill), fill)
            gsparse = jnp.dot(mix[:, :SEQ_ROWS], sparse[:, lanes], precision=HI, preferred_element_type=jnp.float32)
            coef = (2.0 / math.sqrt(vocab)) * gsparse / total[:, lanes]
            parts = jnp.concatenate([*split3(coef), jnp.zeros((128 - 3 * SEQ_ROWS, fill), jnp.bfloat16)], axis=0)
            glogits[:, lanes] = (dot(member, parts) * grown[:, lanes]).astype(jnp.bfloat16)

    out[...] = lax.dot_general(
        features[...], glogits[...], (((0,), (0,)), ((), ())), preferred_element_type=jnp.float32
    ).astype(jnp.bfloat16)


def grad(vocab, ids, positive, scores, spans, total, sparse, grown, features, rows, block):
    slots, depth = features.shape
    columns = grown.shape[1]
    fill = divisor(columns, 2 * block)
    whole = lambda v: vmem(v.shape, lambda i, s, p: (0, 0), **once())
    return pl.pallas_call(
        functools.partial(grad_kernel, fill, vocab),
        out_shape=[
            jax.ShapeDtypeStruct((depth, columns), jnp.bfloat16),
            jax.ShapeDtypeStruct((1, 1), jnp.float32),
        ],
        grid_spec=pltpu.PrefetchScalarGridSpec(
            num_scalar_prefetch=2,
            grid=(depth // rows,),
            in_specs=[
                whole(scores),
                whole(spans),
                whole(total),
                whole(sparse),
                pl.BlockSpec(memory_space=pltpu.VMEM),
                vmem((slots, rows), lambda i, s, p: (0, i)),
            ],
            out_specs=[
                vmem((rows, columns), lambda i, s, p: (s[i], 0)),
                pl.BlockSpec(memory_space=pltpu.SMEM),
            ],
            scratch_shapes=[
                pltpu.VMEM((slots, columns), jnp.bfloat16),
                pltpu.VMEM((SEQ_ROWS, 128), jnp.float32),
            ],
        ),
        compiler_params=pltpu.CompilerParams(vmem_limit_bytes=40 * MIB),
        cost_estimate=pl.CostEstimate(
            flops=2 * slots * depth * columns,
            bytes_accessed=2 * depth * (columns + slots) + 4 * slots * columns,
            transcendentals=0,
        ),
        name="head_grad",
    )(ids, positive, scores, spans, total, sparse, grown, features)


def divisor(size, most):
    return max(b for b in range(128, most + 1, 128) if size % b == 0)


def step(slots, sizes, model_width, vocab, hidden, lengths, positive, norm_gain, head):
    dp_size = sizes["dp"]
    devices = dp_size * sizes["vocab"]
    width = hidden.shape[1]
    columns = head.shape[1]
    block = divisor(columns, 512 if 4 * slots <= 3 * SEQ * lengths.shape[0] else 256)
    chips = dp_size // 2
    rows = chips // 2
    ring = [2 * i for i in range(rows)] + [2 * i + 1 for i in reversed(range(rows))]
    forward, backward = [], []
    for i in range(chips):
        for core in range(2):
            here, after = 2 * ring[i] + core, 2 * ring[(i + 1) % chips] + core
            forward.append((here, after))
            backward.append((after, here))
    swap = [(j, j ^ 1) for j in range(dp_size)]

    table = np.zeros((dp_size, dp_size), np.int32)
    for j in range(dp_size):
        core, here = j % 2, ring.index(j // 2)
        got = [(here, core), (here, 1 - core)]
        for k in range(1, chips // 2):
            got += [(here - k, core), (here + k, core), (here - k, 1 - core), (here + k, 1 - core)]
        got += [(here + chips // 2, core), (here + chips // 2, 1 - core)]
        table[j] = [2 * ring[at % chips] + side for at, side in got]
    order = jnp.asarray(table)[lax.axis_index("dp")]

    at = 0

    def partial(pieces, before, spans=None):
        nonlocal at
        state = logits_step(
            slots, at, model_width, vocab, sizes["vocab"], devices, width, lengths, pieces, order, head, before,
            block, spans,
        )
        at += width * len(pieces)
        return state

    pay, spans = pack(slots, lengths, hidden, norm_gain)
    send = lambda x, pairs: lax.ppermute(x, "dp", pairs)
    up, down = pay, pay
    fresh, state = [(pay,), (send(pay, swap),)], None
    for _ in range(1, chips // 2):
        from_up, from_down = send(up, forward), send(down, backward)
        state = partial(fresh, state)
        up, down, state[1] = lax.optimization_barrier((from_up, from_down, state[1]))
        fresh = [(up,), (down,), (send(up, swap),), (send(down, swap),)]
    cut = (slots + EXTRA) // 32 * 16
    from_up, from_down = send(up[:cut], forward), send(down[cut:], backward)
    state = partial(fresh, state)
    up, down, state[1] = lax.optimization_barrier((from_up, from_down, state[1]))
    across = [(up, down), (send(up, swap), send(down, swap))]
    grown, _, full, total, sparse, scores = partial(across, state, spans)
    scores = lax.all_to_all(scores, ("dp", "vocab"), 0, 0, tiled=True)
    head_grad, loss = grad(vocab, order, positive, scores, spans, total, sparse, grown, full, width, block)
    return loss[0, 0], head_grad


def solution(mesh):
    sizes = {name: mesh.shape[name] for name in ("dp", "vocab")}

    def shards(hidden, lengths, positive, norm_gain, head):
        tokens = hidden.shape[0]
        model_width = hidden.shape[1] * sizes["dp"]
        vocab = head.shape[1] * sizes["dp"] * sizes["vocab"]
        choices = [tokens * 2 // 3, tokens * 3 // 4, tokens]
        used = jnp.sum(lengths)
        which = sum((used > t).astype(jnp.int32) for t in choices[:-1])
        branches = [
            (lambda t: lambda *a: step(t, sizes, model_width, vocab, *a))(t) for t in choices
        ]
        return lax.switch(which, branches, hidden, lengths, positive, norm_gain, head)

    in_specs = (P(None, "dp"), P(), P(), P("dp"), P(None, ("dp", "vocab")))
    out_specs = (P(), P(None, ("dp", "vocab")))
    return jax.shard_map(shards, mesh=mesh, in_specs=in_specs, out_specs=out_specs, check_vma=False)
```
